512 devices in a mesh: row: 16 (over z, y_lo), col: 32 (over x, y_hi, core).
Axes of the slice: x: 4, y: 8 (y_hi: 4, y_lo: 2; y = y_hi * 2 + y_lo), z: 8, core: 2. Of those that a mesh axis runs over, the one named last changes fastest.
Arguments:
- contribution: float32 [4096, 24576], P('row', 'col'), may hold values from -6 to 6
- left_basis: bfloat16 [8, 32, 64, 4096], P(None, 'col', None, 'row'), may hold values from -6 to 6
- left_coef: bfloat16 [8, 32, 64, 4096], P(None, 'col', None, 'row'), may hold values from -0.75 to 0.75
- right_coef: bfloat16 [8, 16, 64, 8192], P(None, 'row', None, 'col'), may hold values from -0.75 to 0.75
- right_basis: bfloat16 [8, 16, 64, 24576], P(None, 'row', None, 'col'), may hold values from -6 to 6
- left_rank: int32 [8, 16], P(None, 'row'), may hold values from 8 to 64
- left_scale: float32 [8, 16], P(None, 'row'), may hold values from 0.08 to 0.8
- right_rank: int32 [8, 32], P(None, 'col'), may hold values from 8 to 64
- right_scale: float32 [8, 32], P(None, 'col'), may hold values from 0.08 to 0.8
- left_owner: int32 [8], replicated, may hold values from 0 to 31
- right_owner: int32 [8], replicated, may hold values from 0 to 15
Outputs:
- updated: float32 [4096, 24576], P('row', 'col')
The draws below stay inside these ranges and needn't reach their ends.
All inputs are finite; a program needn't handle non-finite values.
Results may differ from the reference program's by a relative error of at most 0.0003.
Values may be sent and summed in bfloat16 or wider, within the bound.
A program may use at most 64 MiB of HBM per device.

```python
import math
import jax
import jax.numpy as jnp
from jax import lax

PANEL = 256
RMAX = 64
PANELS = 8
ROW_DEV = 256
COL_DEV = 768
ROW_GROUPS = 16
COL_GROUPS = 32
ROWS = 4096
COLS = 24576
N_ROW = 16
N_COL = 32


def place_ends(drawn, key, low, high):
    index_at = [jax.random.randint(jax.random.fold_in(key, axis), (), 0, length) for axis, length in enumerate(drawn.shape)]
    main_axis = drawn.shape.index(max(drawn.shape))
    next_to = index_at[:main_axis] + [(index_at[main_axis] + 1) % drawn.shape[main_axis]] + index_at[main_axis + 1:]
    return drawn.at[tuple(index_at)].set(low).at[tuple(next_to)].set(high)


def block_scale(stream_key, shape, cuts, least, largest):
    def one(axis_at, blocks):
        steps = jax.random.uniform(jax.random.fold_in(jax.random.fold_in(stream_key, 6), axis_at), (blocks,), jnp.float32, least / len(cuts), largest / len(cuts))
        return jnp.repeat(jnp.exp(steps), shape[axis_at] // blocks).reshape((-1,) + (1,) * (len(shape) - axis_at - 1))

    gain = one(*cuts[0])
    for cut in cuts[1:]:
        gain = gain * one(*cut)
    return gain


def gaussian(stream_key, dims, scale, most, pieces=(), dtype=jnp.bfloat16):
    factor_of = block_scale(stream_key, dims, pieces, -0.22, 0.18) if pieces else 1.0
    result = jax.random.normal(stream_key, dims, jnp.float32) * scale * factor_of
    return jnp.minimum(jnp.maximum(result, -most), most).astype(dtype)


def setup_inputs(seed: int = 0) -> dict:
    streams_of = jax.random.split(jax.random.key(seed), 12)
    return {
        "contribution": gaussian(streams_of[0], (ROWS, COLS), 1.0, 6.0, ((0, 16), (1, 32)), jnp.float32),
        "left_basis": gaussian(streams_of[1], (PANELS, COL_GROUPS, RMAX, ROWS), 1.0, 6.0, ((1, 32), (3, 16))),
        "left_coef": gaussian(streams_of[2], (PANELS, COL_GROUPS, RMAX, ROW_GROUPS * PANEL), RMAX ** -0.5, 0.75, ((1, 32), (3, 16))),
        "right_coef": gaussian(streams_of[3], (PANELS, ROW_GROUPS, RMAX, COL_GROUPS * PANEL), RMAX ** -0.5, 0.75, ((1, 16), (3, 32))),
        "right_basis": gaussian(streams_of[4], (PANELS, ROW_GROUPS, RMAX, COLS), 1.0, 6.0, ((1, 16), (3, 32))),
        "left_rank": place_ends(jax.random.randint(streams_of[5], (PANELS, ROW_GROUPS), 8, RMAX + 1), jax.random.fold_in(streams_of[5], 1), 8, RMAX).astype(jnp.int32),
        "left_scale": jnp.clip(jnp.exp(math.log(0.8) - 2.3025851 * jax.random.uniform(streams_of[6], (PANELS, ROW_GROUPS), jnp.float32) ** block_scale(streams_of[6], (PANELS, ROW_GROUPS), ((1, 16),), -0.2, 0.2)), 0.08, 0.8),
        "right_rank": place_ends(jax.random.randint(streams_of[7], (PANELS, COL_GROUPS), 8, RMAX + 1), jax.random.fold_in(streams_of[7], 1), 8, RMAX).astype(jnp.int32),
        "right_scale": jnp.clip(jnp.exp(math.log(0.8) - 2.3025851 * jax.random.uniform(streams_of[8], (PANELS, COL_GROUPS), jnp.float32) ** block_scale(streams_of[8], (PANELS, COL_GROUPS), ((1, 32),), -0.2, 0.2)), 0.08, 0.8),
        "left_owner": place_ends(jax.random.randint(streams_of[9], (PANELS,), 0, COL_GROUPS), jax.random.fold_in(streams_of[9], 1), 0, COL_GROUPS - 1).astype(jnp.int32),
        "right_owner": place_ends(jax.random.randint(streams_of[10], (PANELS,), 0, ROW_GROUPS), jax.random.fold_in(streams_of[10], 1), 0, ROW_GROUPS - 1).astype(jnp.int32),
    }


def reference(contribution, left_basis, left_coef, right_coef, right_basis, left_rank, left_scale, right_rank, right_scale, left_owner, right_owner):
    hp = lax.Precision.HIGHEST
    slots = jnp.arange(RMAX)
    total = jnp.zeros((N_ROW, ROW_DEV, N_COL, COL_DEV), jnp.float32)
    for panel in range(PANELS):
        lo = left_owner[panel]
        ro = right_owner[panel]
        xb = left_basis[panel][lo].astype(jnp.float32).reshape(RMAX, N_ROW, ROW_DEV)
        yb = left_coef[panel][lo].astype(jnp.float32).reshape(RMAX, N_ROW, PANEL)
        zb = right_coef[panel][ro].astype(jnp.float32).reshape(RMAX, N_COL, PANEL)
        wb = right_basis[panel][ro].astype(jnp.float32).reshape(RMAX, N_COL, COL_DEV)
        lweight = jnp.where(slots[None, :] < left_rank[panel][:, None], left_scale[panel][:, None], jnp.float32(0.0))
        rweight = jnp.where(slots[None, :] < right_rank[panel][:, None], right_scale[panel][:, None], jnp.float32(0.0))
        xb = xb * lweight.T[:, :, None]
        zb = zb * rweight.T[:, :, None]
        core = jnp.einsum('kip,ljp->ijkl', yb, zb, precision=hp)
        middle = jnp.einsum('ijkl,ljc->ijkc', core, wb, precision=hp)
        total = total + jnp.einsum('kir,ijkc->irjc', xb, middle, precision=hp)
    return contribution - total.reshape(N_ROW * ROW_DEV, N_COL * COL_DEV)
```

```python
import jax
import jax.numpy as jnp
from jax import lax
from jax.experimental import pallas as pl
from jax.experimental.pallas import tpu as pltpu
from jax.sharding import PartitionSpec as P

MESH = pl.DeviceIdType.MESH
BF16, F32 = jnp.bfloat16, jnp.float32
PANELS, RANK, WIDE = 8, 64, 256
ROWS_OUT, COLS_OUT = 256, 768
ZS, XS, HS = 8, 4, 4
N_SEND, N_RECV = 112, 112


def ring(value, size):
    return lax.rem(value + 4 * size, size)


def flat_dot(left, right, dims):
    return lax.dot_general(left, right, (dims, ((), ())), preferred_element_type=F32)


def split(value):
    high = value.astype(BF16)
    return high, (value - high.astype(F32)).astype(BF16)


def kernel(
    lowner, rowner, lrank, lscale, rrank, rscale,
    lbasis, lcoef, rcoef, rbasis,
    out,
    own, from_lo, from_hi, right, yswap, yhold,
    lown, lother, lpick, lx, lhome, ly, lquarter, left,
    mid_high, mid_low,
    load_sem, send_sem, recv_sem,
):
    row, col = lax.axis_index("row"), lax.axis_index("col")
    z, q = row // 2, lax.rem(row, 2)
    x, h, core = col // 8, lax.rem(col // 2, 4), lax.rem(col, 2)

    def at_row(zz, qq):
        return (zz * 2 + qq, col)

    def at_col(xx, hh, cc):
        return (row, (xx * 4 + hh) * 2 + cc)

    z_up, z_dn = at_row(ring(z + 1, ZS), q), at_row(ring(z - 1, ZS), q)
    y_mate, core_mate = at_row(z, 1 - q), at_col(x, h, 1 - core)
    x_peers = [at_col(ring(x + d, XS), h, core) for d in (1, 2, 3)]
    h_peers = [at_col(x, ring(h + d, HS), core) for d in (1, 2, 3)]
    everyone = [z_up, z_dn, y_mate, core_mate] + x_peers + h_peers

    loads = [
        pltpu.make_async_copy(rcoef.at[:, 0], own.at[:, 0], load_sem.at[0]),
        pltpu.make_async_copy(lbasis.at[:, 0], lown.at[0], load_sem.at[4]),
        pltpu.make_async_copy(lcoef.at[:, 0], lown.at[1], load_sem.at[5]),
    ] + [
        pltpu.make_async_copy(
            rbasis.at[:, 0, :, pl.ds(WIDE * (u - 1), WIDE)], own.at[:, u], load_sem.at[u]
        )
        for u in (1, 2, 3)
    ]
    for load in loads:
        load.start()

    barrier = pltpu.get_barrier_semaphore()
    for peer in everyone:
        pl.semaphore_signal(barrier, inc=1, device_id=peer, device_id_type=MESH)
    pl.semaphore_wait(barrier, len(everyone))
    for load in loads:
        load.wait()

    sent, slots = [], {}

    def send(src, dst, key, peer):
        slot = slots.setdefault(key, len(slots))
        copy = pltpu.make_async_remote_copy(
            src_ref=src, dst_ref=dst, send_sem=send_sem.at[len(sent)],
            recv_sem=recv_sem.at[slot], device_id=peer, device_id_type=MESH,
        )
        copy.start()
        sent.append(copy)

    def arrived(dst, key):
        slot = slots.setdefault(key, len(slots))
        pltpu.make_async_remote_copy(
            src_ref=dst, dst_ref=dst, send_sem=send_sem.at[0],
            recv_sem=recv_sem.at[slot], device_id=core_mate, device_id_type=MESH,
        ).wait_recv()

    units = [2 * (1 - q), 2 * (1 - q) + 1, 2 * q, 2 * q + 1]

    def collect(u, step):
        odd = u % 2
        for up in (True, False):
            long = (odd == 0) == up
            if step == 1 and not long:
                continue
            bufs = from_lo if up else from_hi
            panel = ring(z + (5 - step if up else step - 5), ZS)
            peer = z_up if up else z_dn
            target = bufs.at[step - 1, u]
            if step == 1 or (step == 2 and not long):
                send(own.at[panel, units[u]], target, ("c", up, step, u), peer)
            else:
                held = bufs.at[step - 2, u]
                arrived(held, ("c", up, step - 1, u))
                mine = rowner[panel] // 2 == z
                held[...] = jnp.where(mine, own[panel, units[u]], held[...])
                send(held, target, ("c", up, step, u), peer)

    def home(u):
        arrived(from_lo.at[3, u], ("c", True, 4, u))
        arrived(from_hi.at[3, u], ("c", False, 4, u))
        far = ring(rowner[z] // 2 - z, ZS)
        limit = 4 if u % 2 == 0 else 5
        picked = jnp.where(far >= limit, from_lo[3, u], from_hi[3, u])
        picked = jnp.where(far == 0, own[z, units[u]], picked)
        e = u % 2
        if u < 2:
            yhold[e] = picked
            send(yhold.at[e], yswap.at[e], ("y", e), y_mate)
        else:
            arrived(yswap.at[e], ("y", e))
            right[z, units[u]] = jnp.where(lax.rem(rowner[z], 2) == q, picked, yswap[e])
            ref = right.at[z, units[u]]
            send(ref, ref, ("g", True, 1, e), z_up)
            send(ref, ref, ("g", False, 1, e), z_dn)
            send(ref, ref, ("f", 0, e), y_mate)

    def spread(up, d, e):
        reach = 4 if (e == 0) == up else 3
        if d > reach:
            return
        panel = ring(z - d if up else z + d, ZS)
        ref = right.at[panel, units[2 + e]]
        arrived(ref, ("g", up, d, e))
        if d < reach:
            send(ref, ref, ("g", up, d + 1, e), z_up if up else z_dn)
        send(ref, ref, ("f", (-d if up else d) % ZS, e), y_mate)

    def left_core():
        send(lown.at[1 - core], lother, ("l", 0), core_mate)

    def left_x():
        arrived(lother, ("l", 0))
        for p in range(PANELS):
            mine = lax.rem(lowner[p], 2) == core
            lpick[p // 2, p % 2] = jnp.where(mine, lown[core, p], lother[p])
        for d in (1, 2, 3):
            to = ring(x + d, XS)
            send(lpick.at[to], lx.at[d - 1], ("lx", d), x_peers[d - 1])

    def left_h():
        for d in (1, 2, 3):
            arrived(lx.at[d - 1], ("lx", d))
        for i in range(2):
            away = ring(x - lowner[2 * x + i] // 8, XS)
            value = lpick[x, i]
            for d in (1, 2, 3):
                value = jnp.where(away == d, lx[d - 1, i], value)
            for j in range(2):
                lhome[2 * i + j] = value[32 * j:32 * (j + 1)]
        for d in (1, 2, 3):
            to = ring(h + d, HS)
            send(lhome.at[to], ly.at[d - 1], ("ly", d), h_peers[d - 1])

    def left_hback():
        for d in (1, 2, 3):
            arrived(ly.at[d - 1], ("ly", d))
        away = ring(h - lax.rem(lowner[2 * x + h // 2] // 2, 4), HS)
        value = lhome[h]
        for d in (1, 2, 3):
            value = jnp.where(away == d, ly[d - 1], value)
        left[core, x, h] = value
        ref = left.at[core, x, h]
        for d in (1, 2, 3):
            send(ref, ref, ("lh", d), h_peers[d - 1])

    def left_xback():
        for d in (1, 2, 3):
            arrived(left.at[core, x, ring(h - d, HS)], ("lh", d))
        ref = left.at[core, x]
        for d in (1, 2, 3):
            send(ref, ref, ("lb", d), x_peers[d - 1])
        send(ref, ref, ("lc", 0), core_mate)

    def left_coreback():
        for d in (1, 2, 3):
            ref = left.at[core, ring(x - d, XS)]
            arrived(ref, ("lb", d))
            send(ref, ref, ("lc", d), core_mate)

    def left_end():
        for d in range(4):
            arrived(left.at[1 - core, ring(x - d, XS)], ("lc", d))

    left_core()
    for tick in range(1, 9):
        if tick == 2:
            left_x()
        if tick == 4:
            left_h()
        if tick == 6:
            left_hback()
        if tick == 8:
            left_xback()
        for u in range(4):
            step = tick - u
            if 1 <= step <= 4:
                collect(u, step)
            elif step == 5:
                home(u)
    for d in (1, 2, 3, 4):
        if d == 3:
            left_coreback()
        for e in (0, 1):
            for up in (True, False):
                spread(up, d, e)
    left_end()
    for e in (0, 1):
        for offset in range(ZS):
            arrived(right.at[ring(z + offset, ZS), 2 * (1 - q) + e], ("f", offset, e))

    slot_row = lax.broadcasted_iota(jnp.int32, (RANK, RANK), 0)
    slot_col = lax.broadcasted_iota(jnp.int32, (RANK, RANK), 1)
    for p in range(PANELS):
        coef = left[1, p // 2, pl.ds(2 * (p % 2), 2)].reshape(RANK, WIDE)
        small = flat_dot(coef, right[p, 0], ((1,), (1,)))
        keep = (slot_row < lrank[p, 0]) & (slot_col < rrank[p, 0])
        small = jnp.where(keep, small * (lscale[p, 0] * rscale[p, 0]), 0.0)
        small_high, small_low = split(small)
        for u in (1, 2, 3):
            wide = right[p, u]
            middle = flat_dot(small_high, wide, ((1,), (0,))) + flat_dot(small_low, wide, ((1,), (0,)))
            high, low = split(middle)
            place = pl.ds(RANK * p, RANK), pl.ds(WIDE * (u - 1), WIDE)
            mid_high[place] = high
            mid_low[place] = low
    basis = left[0].reshape(PANELS * RANK, WIDE)
    out[...] = flat_dot(basis, mid_high[...], ((0,), (0,))) + flat_dot(basis, mid_low[...], ((0,), (0,)))

    for copy in sent:
        copy.wait_send()
    assert len(sent) <= N_SEND and len(slots) <= N_RECV, (len(sent), len(slots))


def shards(
    contribution, left_basis, left_coef, right_coef, right_basis,
    left_rank, left_scale, right_rank, right_scale, left_owner, right_owner,
):
    smem = pl.BlockSpec(memory_space=pltpu.SMEM)
    hbm = pl.BlockSpec(memory_space=pl.ANY)
    unit = (RANK, WIDE)
    update = pl.pallas_call(
        kernel,
        out_shape=jax.ShapeDtypeStruct((ROWS_OUT, COLS_OUT), F32),
        in_specs=[smem] * 6 + [hbm] * 4,
        out_specs=pl.BlockSpec(memory_space=pltpu.VMEM),
        scratch_shapes=[
            pltpu.VMEM((PANELS, 4) + unit, BF16),
            pltpu.VMEM((4, 4) + unit, BF16),
            pltpu.VMEM((4, 4) + unit, BF16),
            pltpu.VMEM((PANELS, 4) + unit, BF16),
            pltpu.VMEM((2,) + unit, BF16),
            pltpu.VMEM((2,) + unit, BF16),
            pltpu.VMEM((2, PANELS) + unit, BF16),
            pltpu.VMEM((PANELS,) + unit, BF16),
            pltpu.VMEM((XS, 2) + unit, BF16),
            pltpu.VMEM((3, 2) + unit, BF16),
            pltpu.VMEM((HS, 32, WIDE), BF16),
            pltpu.VMEM((3, 32, WIDE), BF16),
            pltpu.VMEM((32, WIDE), BF16),
            pltpu.VMEM((2, XS, HS, 32, WIDE), BF16),
            pltpu.VMEM((PANELS * RANK, COLS_OUT), BF16),
            pltpu.VMEM((PANELS * RANK, COLS_OUT), BF16),
            pltpu.SemaphoreType.DMA((6,)),
            pltpu.SemaphoreType.DMA((N_SEND,)),
            pltpu.SemaphoreType.DMA((N_RECV,)),
        ],
        compiler_params=pltpu.CompilerParams(collective_id=0, has_side_effects=True),
    )(
        left_owner, right_owner, left_rank, left_scale, right_rank, right_scale,
        left_basis, left_coef, right_coef, right_basis,
    )
    return contribution - update


def solution(mesh):
    return jax.shard_map(
        shards,
        mesh=mesh,
        in_specs=(
            P("row", "col"),
            P(None, "col", None, "row"),
            P(None, "col", None, "row"),
            P(None, "row", None, "col"),
            P(None, "row", None, "col"),
            P(None, "row"),
            P(None, "row"),
            P(None, "col"),
            P(None, "col"),
            P(),
            P(),
        ),
        out_specs=P("row", "col"),
        check_vma=False,
    )
```

```python
import jax
import jax.numpy as jnp
from jax import lax
from jax.experimental import pallas as pl
from jax.experimental.pallas import tpu as pltpu
from jax.sharding import PartitionSpec as P

MESH = pl.DeviceIdType.MESH
BF16, F32 = jnp.bfloat16, jnp.float32
PANELS, RANK, WIDE = 8, 64, 256
ROWS_OUT, COLS_OUT = 256, 768
ZS, XS, HS = 8, 4, 4
FAR_FIRST = (4, 3, 5, 2, 6, 1, 7)
NEAR, FAR = (0, 1, 7, 2, 6), (3, 5, 4)


def ring(value, size):
    return lax.rem(value + 4 * size, size)


def flat_dot(left, right, dims):
    return lax.dot_general(left, right, (dims, ((), ())), preferred_element_type=F32)


def split(value):
    high = value.astype(BF16)
    return high, (value - high.astype(F32)).astype(BF16)


def kernel(
    lowner, rowner, lrank, lscale, rrank, rscale,
    lbasis, lcoef, rcoef, rbasis,
    out,
    own, yin, zout, zin, right,
    lown, lother, lpick, lx, lhome, ly, left,
    basis, mid_high, mid_low,
    load_sem, send_sem, y_sem, z_sem, g_sem, f_sem, l_sem,
):
    row, col = lax.axis_index("row"), lax.axis_index("col")
    z, q = row // 2, lax.rem(row, 2)
    x, h, core = col // 8, lax.rem(col // 2, 4), lax.rem(col, 2)

    def at_z(offset):
        return (ring(z + offset, ZS) * 2 + q, col)

    def at_col(xx, hh, cc):
        return (row, (xx * 4 + hh) * 2 + cc)

    y_mate, core_mate = (z * 2 + 1 - q, col), at_col(x, h, 1 - core)
    x_peers = [at_col(ring(x + d, XS), h, core) for d in (1, 2, 3)]
    h_peers = [at_col(x, ring(h + d, HS), core) for d in (1, 2, 3)]
    everyone = [at_z(o) for o in FAR_FIRST] + [y_mate, core_mate] + x_peers + h_peers

    loads = [
        pltpu.make_async_copy(rcoef.at[:, 0], own.at[:, 0], load_sem.at[0]),
        pltpu.make_async_copy(lbasis.at[:, 0], lown.at[0], load_sem.at[4]),
        pltpu.make_async_copy(lcoef.at[:, 0], lown.at[1], load_sem.at[5]),
    ] + [
        pltpu.make_async_copy(
            rbasis.at[:, 0, :, pl.ds(WIDE * (u - 1), WIDE)], own.at[:, u], load_sem.at[u]
        )
        for u in (1, 2, 3)
    ]
    for load in loads:
        load.start()

    barrier = pltpu.get_barrier_semaphore()
    for peer in everyone:
        pl.semaphore_signal(barrier, inc=1, device_id=peer, device_id_type=MESH)
    for load in loads:
        load.wait()
    pl.semaphore_wait(barrier, len(everyone))

    def send(src, dst, sem, peer, group):
        pltpu.make_async_remote_copy(
            src_ref=src, dst_ref=dst, send_sem=send_sem.at[group],
            recv_sem=sem, device_id=peer, device_id_type=MESH,
        ).start()

    def wait(ref, sem):
        pltpu.make_async_remote_copy(
            src_ref=ref, dst_ref=ref, send_sem=send_sem.at[0],
            recv_sem=sem, device_id=core_mate, device_id_type=MESH,
        ).wait_recv()

    def wait_sent(ref, group):
        pltpu.make_async_remote_copy(
            src_ref=ref, dst_ref=ref, send_sem=send_sem.at[group],
            recv_sem=z_sem, device_id=core_mate, device_id_type=MESH,
        ).wait_send()

    stay, leave = pl.ds(2 * q, 2), pl.ds(2 * (1 - q), 2)

    def left_core():
        send(lown.at[1 - core], lother, l_sem.at[0], core_mate, 1)

    def left_x():
        wait(lother, l_sem.at[0])
        for p in range(PANELS):
            mine = lax.rem(lowner[p], 2) == core
            lpick[p // 2, p % 2] = jnp.where(mine, lown[core, p], lother[p])
        for d in (2, 1, 3):
            send(lpick.at[ring(x + d, XS)], lx.at[d - 1], l_sem.at[1], x_peers[d - 1], 2)

    def left_h():
        wait(lx, l_sem.at[1])
        for i in range(2):
            away = ring(x - lowner[2 * x + i] // 8, XS)
            value = lpick[x, i]
            for d in (1, 2, 3):
                value = jnp.where(away == d, lx[d - 1, i], value)
            for j in range(2):
                lhome[2 * i + j] = value[32 * j:32 * (j + 1)]
        for d in (2, 1, 3):
            send(lhome.at[ring(h + d, HS)], ly.at[d - 1], l_sem.at[2], h_peers[d - 1], 3)

    def left_hback():
        wait(ly, l_sem.at[2])
        away = ring(h - lax.rem(lowner[2 * x + h // 2] // 2, 4), HS)
        value = lhome[h]
        for d in (1, 2, 3):
            value = jnp.where(away == d, ly[d - 1], value)
        left[core, x, h] = value
        ref = left.at[core, x, h]
        for d in (2, 1, 3):
            send(ref, ref, l_sem.at[3], h_peers[d - 1], 4)

    def left_xback():
        wait(ly, l_sem.at[3])
        ref = left.at[core, x]
        for d in (2, 1, 3):
            send(ref, ref, l_sem.at[3 + d], x_peers[d - 1], 5)
        send(ref, ref, l_sem.at[7], core_mate, 6)

    def left_coreback():
        for d in (1, 3, 2):
            ref = left.at[core, ring(x - d, XS)]
            wait(ref, l_sem.at[3 + d])
            send(ref, ref, l_sem.at[7], core_mate, 6)

    def left_end():
        wait(lown.at[0], l_sem.at[7])

    def pick(offset):
        panel = ring(z + offset, ZS)
        wait(yin.at[offset], y_sem.at[offset])
        mine = lax.rem(rowner[panel], 2) == q
        return jnp.where(mine, own[panel, stay], yin[offset])

    def scatter(offset):
        zout[offset - 1] = pick(offset)
        send(zout.at[offset - 1], zin.at[offset], z_sem, at_z(offset), 7)

    def mine_at(offset):
        return right.at[ring(z + offset, ZS), stay]

    def forward(offset):
        send(mine_at(offset), mine_at(offset), f_sem.at[int(offset in FAR)], y_mate, 8)

    def received(offset):
        wait(mine_at(offset), g_sem.at[offset])

    left_core()
    for o in FAR_FIRST + (0,):
        send(own.at[ring(z + o, ZS), leave], yin.at[o], y_sem.at[o], y_mate, 0)
    left_x()
    for o in FAR_FIRST[:4]:
        scatter(o)
    left_h()
    for o in FAR_FIRST[4:]:
        scatter(o)
    zin[0] = pick(0)
    left_hback()
    wait(zin.at[pl.ds(1, 7)], z_sem)
    right[z, stay] = zin[ring(z - rowner[z] // 2, ZS)]
    home = mine_at(0)
    for d in (2, -2, 1, -1):
        send(home, home, g_sem.at[-d % ZS], at_z(d), 9)
    forward(0)
    left_xback()
    for d in (2, -2):
        received(-d % ZS)
        ref = mine_at(-d)
        e = 0 if d > 0 else 1
        one = right.at[ring(z - d, ZS), 2 * q + e]
        send(one, one, g_sem.at[4], at_z(d), 11)
        send(ref, ref, g_sem.at[(-d - d // 2) % ZS], at_z(d // 2), 10)
        forward(-d % ZS)
    for o in (1, 7):
        received(o)
        forward(o)
    left_coreback()
    for o in FAR:
        received(o)
        forward(o)
    left_end()

    slot_row = lax.broadcasted_iota(jnp.int32, (RANK, RANK), 0)
    slot_col = lax.broadcasted_iota(jnp.int32, (RANK, RANK), 1)

    def products(offsets, start):
        for i, o in enumerate(offsets):
            p = ring(z + o, ZS)
            pair = p // 2, pl.ds(2 * lax.rem(p, 2), 2)
            rows = pl.ds(RANK * (start + i), RANK)
            basis[rows, :] = left[(0,) + pair].reshape(RANK, WIDE)
            coef = left[(1,) + pair].reshape(RANK, WIDE)
            small = flat_dot(coef, right[p, 0], ((1,), (1,)))
            keep = (slot_row < lrank[0, p]) & (slot_col < rrank[0, p])
            small = jnp.where(keep, small * (lscale[0, p] * rscale[0, p]), 0.0)
            small_high, small_low = split(small)
            for u in (1, 2, 3):
                wide = right[p, u]
                middle = flat_dot(small_high, wide, ((1,), (0,))) + flat_dot(small_low, wide, ((1,), (0,)))
                high, low = split(middle)
                place = rows, pl.ds(WIDE * (u - 1), WIDE)
                mid_high[place] = high
                mid_low[place] = low
        rows = pl.ds(RANK * start, RANK * len(offsets))
        lhs = basis[rows, :]
        return flat_dot(lhs, mid_high[rows, :], ((0,), (0,))) + flat_dot(lhs, mid_low[rows, :], ((0,), (0,)))

    wait(zin.at[pl.ds(0, 5)], f_sem.at[0])
    out[...] = products(NEAR, 0)
    wait(zin.at[pl.ds(0, 3)], f_sem.at[1])
    out[...] += products(FAR, len(NEAR))

    wait_sent(lown.at[0], 1)
    wait_sent(lx, 2)
    wait_sent(ly, 3)
    wait_sent(ly, 4)
    wait_sent(lx, 5)
    wait_sent(lown.at[0], 6)
    wait_sent(zin, 0)
    wait_sent(zout, 7)
    wait_sent(zin, 8)
    wait_sent(zin.at[pl.ds(0, 4)], 9)
    wait_sent(zin.at[pl.ds(0, 2)], 10)
    wait_sent(zin.at[0], 11)


def shards(
    contribution, left_basis, left_coef, right_coef, right_basis,
    left_rank, left_scale, right_rank, right_scale, left_owner, right_owner,
):
    smem = pl.BlockSpec(memory_space=pltpu.SMEM)
    hbm = pl.BlockSpec(memory_space=pl.ANY)
    unit = (RANK, WIDE)
    update = pl.pallas_call(
        kernel,
        out_shape=jax.ShapeDtypeStruct((ROWS_OUT, COLS_OUT), F32),
        in_specs=[smem] * 6 + [hbm] * 4,
        out_specs=pl.BlockSpec(memory_space=pltpu.VMEM),
        scratch_shapes=[
            pltpu.VMEM((PANELS, 4) + unit, BF16),
            pltpu.VMEM((ZS, 2) + unit, BF16),
            pltpu.VMEM((ZS - 1, 2) + unit, BF16),
            pltpu.VMEM((ZS, 2) + unit, BF16),
            pltpu.VMEM((PANELS, 4) + unit, BF16),
            pltpu.VMEM((2, PANELS) + unit, BF16),
            pltpu.VMEM((PANELS,) + unit, BF16),
            pltpu.VMEM((XS, 2) + unit, BF16),
            pltpu.VMEM((3, 2) + unit, BF16),
            pltpu.VMEM((HS, 32, WIDE), BF16),
            pltpu.VMEM((3, 32, WIDE), BF16),
            pltpu.VMEM((2, XS, HS, 32, WIDE), BF16),
            pltpu.VMEM((PANELS * RANK, WIDE), BF16),
            pltpu.VMEM((PANELS * RANK, COLS_OUT), BF16),
            pltpu.VMEM((PANELS * RANK, COLS_OUT), BF16),
            pltpu.SemaphoreType.DMA((6,)),
            pltpu.SemaphoreType.DMA((12,)),
            pltpu.SemaphoreType.DMA((ZS,)),
            pltpu.SemaphoreType.DMA,
            pltpu.SemaphoreType.DMA((ZS,)),
            pltpu.SemaphoreType.DMA((2,)),
            pltpu.SemaphoreType.DMA((8,)),
        ],
        compiler_params=pltpu.CompilerParams(collective_id=0, has_side_effects=True),
    )(
        left_owner, right_owner, left_rank.T, left_scale.T, right_rank.T, right_scale.T,
        left_basis, left_coef, right_coef, right_basis,
    )
    return contribution - update


def solution(mesh):
    return jax.shard_map(
        shards,
        mesh=mesh,
        in_specs=(
            P("row", "col"),
            P(None, "col", None, "row"),
            P(None, "col", None, "row"),
            P(None, "row", None, "col"),
            P(None, "row", None, "col"),
            P(None, "row"),
            P(None, "row"),
            P(None, "col"),
            P(None, "col"),
            P(),
            P(),
        ),
        out_specs=P("row", "col"),
        check_vma=False,
    )
```

```python
import jax
import jax.numpy as jnp
from jax import lax
from jax.experimental import pallas as pl
from jax.experimental.pallas import tpu as pltpu
from jax.sharding import PartitionSpec as P

MESH = pl.DeviceIdType.MESH
BF16, F32 = jnp.bfloat16, jnp.float32
PANELS, RANK, WIDE = 8, 64, 256
ROWS_OUT, COLS_OUT = 256, 768
ZS, XS, HS = 8, 4, 4
FAR_FIRST = (4, 3, 5, 2, 6, 1, 7)
NEAR, FAR = (0, 1, 7, 2, 6), (3, 5)
F_SLOT = {0: 0, 1: 1, 2: 1, 6: 1, 3: 2, 5: 2, 4: 3}


def ring(value, size):
    return lax.rem(value + 4 * size, size)


def flat_dot(left, right, dims):
    return lax.dot_general(left, right, (dims, ((), ())), preferred_element_type=F32)


def split(value):
    high = value.astype(BF16)
    return high, (value - high.astype(F32)).astype(BF16)


def kernel(
    lowner, rowner, lrank, lscale, rrank, rscale,
    lbasis, lcoef, rcoef, rbasis,
    out,
    own, yin, zout, zin, right,
    lown, lother, lpick, lx, lhome, ly, left,
    basis, mid_high, mid_low,
    load_sem, send_sem, y_sem, z_sem, g_sem, f_sem, l_sem,
):
    row, col = lax.axis_index("row"), lax.axis_index("col")
    z, q = row // 2, lax.rem(row, 2)
    x, h, core = col // 8, lax.rem(col // 2, 4), lax.rem(col, 2)

    def at_z(offset):
        return (ring(z + offset, ZS) * 2 + q, col)

    def at_col(xx, hh, cc):
        return (row, (xx * 4 + hh) * 2 + cc)

    y_mate, core_mate = (z * 2 + 1 - q, col), at_col(x, h, 1 - core)
    x_peers = [at_col(ring(x + d, XS), h, core) for d in (1, 2, 3)]
    h_peers = [at_col(x, ring(h + d, HS), core) for d in (1, 2, 3)]
    everyone = [at_z(o) for o in FAR_FIRST] + [y_mate, core_mate] + x_peers + h_peers

    loads = [
        pltpu.make_async_copy(rcoef.at[:, 0], own.at[:, 0], load_sem.at[0]),
        pltpu.make_async_copy(lbasis.at[:, 0], lown.at[0], load_sem.at[4]),
        pltpu.make_async_copy(lcoef.at[:, 0], lown.at[1], load_sem.at[5]),
    ] + [
        pltpu.make_async_copy(
            rbasis.at[:, 0, :, pl.ds(WIDE * (u - 1), WIDE)], own.at[:, u], load_sem.at[u]
        )
        for u in (1, 2, 3)
    ]
    for load in loads:
        load.start()

    barrier = pltpu.get_barrier_semaphore()
    for peer in everyone:
        pl.semaphore_signal(barrier, inc=1, device_id=peer, device_id_type=MESH)
    for load in loads:
        load.wait()
    pl.semaphore_wait(barrier, len(everyone))

    def send(src, dst, sem, peer, group):
        pltpu.make_async_remote_copy(
            src_ref=src, dst_ref=dst, send_sem=send_sem.at[group],
            recv_sem=sem, device_id=peer, device_id_type=MESH,
        ).start()

    def wait(ref, sem):
        pltpu.make_async_remote_copy(
            src_ref=ref, dst_ref=ref, send_sem=send_sem.at[0],
            recv_sem=sem, device_id=core_mate, device_id_type=MESH,
        ).wait_recv()

    def wait_sent(ref, group):
        pltpu.make_async_remote_copy(
            src_ref=ref, dst_ref=ref, send_sem=send_sem.at[group],
            recv_sem=z_sem, device_id=core_mate, device_id_type=MESH,
        ).wait_send()

    stay, leave = pl.ds(2 * q, 2), pl.ds(2 * (1 - q), 2)

    def left_core():
        send(lown.at[1 - core], lother, l_sem.at[0], core_mate, 1)

    def left_x():
        wait(lother, l_sem.at[0])
        for p in range(PANELS):
            mine = lax.rem(lowner[p], 2) == core
            lpick[p // 2, p % 2] = jnp.where(mine, lown[core, p], lother[p])
        for d in (2, 1, 3):
            send(lpick.at[ring(x + d, XS)], lx.at[d - 1], l_sem.at[1], x_peers[d - 1], 2)

    def left_h():
        wait(lx, l_sem.at[1])
        for i in range(2):
            away = ring(x - lowner[2 * x + i] // 8, XS)
            value = lpick[x, i]
            for d in (1, 2, 3):
                value = jnp.where(away == d, lx[d - 1, i], value)
            for j in range(2):
                lhome[2 * i + j] = value[32 * j:32 * (j + 1)]
        for d in (2, 1, 3):
            send(lhome.at[ring(h + d, HS)], ly.at[d - 1], l_sem.at[2], h_peers[d - 1], 3)

    def left_hback():
        wait(ly, l_sem.at[2])
        away = ring(h - lax.rem(lowner[2 * x + h // 2] // 2, 4), HS)
        value = lhome[h]
        for d in (1, 2, 3):
            value = jnp.where(away == d, ly[d - 1], value)
        left[core, x, h] = value
        ref = left.at[core, x, h]
        for d in (2, 1, 3):
            send(ref, ref, l_sem.at[3], h_peers[d - 1], 4)

    def left_xback():
        wait(ly, l_sem.at[3])
        ref = left.at[core, x]
        for d in (2, 1, 3):
            send(ref, ref, l_sem.at[3 + d], x_peers[d - 1], 5)
        send(ref, ref, l_sem.at[7], core_mate, 6)

    def left_coreback():
        for d in (1, 3, 2):
            ref = left.at[core, ring(x - d, XS)]
            wait(ref, l_sem.at[3 + d])
            send(ref, ref, l_sem.at[7], core_mate, 6)

    def left_end():
        wait(lown.at[0], l_sem.at[7])

    def keep_at(offset, e):
        return right.at[ring(z + offset, ZS), 2 * q + e]

    def scatter(offset):
        panel = ring(z + offset, ZS)
        mine = lax.rem(rowner[panel], 2) == q
        for e in (0, 1):
            wait(yin.at[offset, e], y_sem.at[offset, e])
            value = jnp.where(mine, own[panel, 2 * q + e], yin[offset, e])
            if offset:
                zout[offset - 1, e] = value
                send(zout.at[offset - 1, e], zin.at[offset, e], z_sem, at_z(offset), 7)
            else:
                zin[0, e] = value

    def relay(offset, e, to):
        ref = keep_at(offset, e)
        send(ref, ref, g_sem.at[(offset - to) % ZS, e], at_z(to), 9)

    def forward(offset, e):
        ref = keep_at(offset, e)
        send(ref, ref, f_sem.at[F_SLOT[offset]], y_mate, 8)

    def received(offset, e):
        wait(keep_at(offset, e), g_sem.at[offset, e])

    left_core()
    for o in FAR_FIRST + (0,):
        for e in (0, 1):
            send(own.at[ring(z + o, ZS), 2 * (1 - q) + e], yin.at[o, e], y_sem.at[o, e], y_mate, 0)
    left_x()
    for o in FAR_FIRST[:4]:
        scatter(o)
    left_h()
    for o in FAR_FIRST[4:] + (0,):
        scatter(o)
    left_hback()
    wait(zin.at[pl.ds(1, 7)], z_sem)
    right[z, stay] = zin[ring(z - rowner[z] // 2, ZS)]
    for e in (0, 1):
        forward(0, e)
        relay(0, e, 2)
        relay(0, 1 - e, -2)
    for e in (0, 1):
        relay(0, e, 1)
        relay(0, 1 - e, -1)
    other = right.at[z, leave]
    wait(other, f_sem.at[F_SLOT[0]])
    for d in (1, -1):
        send(other, other, f_sem.at[F_SLOT[1]], at_z(d), 10)
    left_xback()
    for turn in (0, 1):
        for o, step, e in ((6, 1, turn), (2, -1, 1 - turn)):
            received(o, e)
            if turn == 0:
                relay(o, e, 2 * step)
            relay(o, e, step)
            forward(o, e)
    left_coreback()
    for e in (0, 1):
        for o in (7, 1):
            received(o, e)
    for turn in (0, 1):
        for o, e in ((5, turn), (3, 1 - turn)):
            received(o, e)
            forward(o, e)
    for e in (0, 1):
        received(4, e)
        forward(4, e)
    left_end()

    slot_row = lax.broadcasted_iota(jnp.int32, (RANK, RANK), 0)
    slot_col = lax.broadcasted_iota(jnp.int32, (RANK, RANK), 1)

    def products(offsets, start):
        for i, o in enumerate(offsets):
            p = ring(z + o, ZS)
            pair = p // 2, pl.ds(2 * lax.rem(p, 2), 2)
            rows = pl.ds(RANK * (start + i), RANK)
            basis[rows, :] = left[(0,) + pair].reshape(RANK, WIDE)
            coef = left[(1,) + pair].reshape(RANK, WIDE)
            small = flat_dot(coef, right[p, 0], ((1,), (1,)))
            keep = (slot_row < lrank[0, p]) & (slot_col < rrank[0, p])
            small = jnp.where(keep, small * (lscale[0, p] * rscale[0, p]), 0.0)
            small_high, small_low = split(small)
            for u in (1, 2, 3):
                wide = right[p, u]
                middle = flat_dot(small_high, wide, ((1,), (0,))) + flat_dot(small_low, wide, ((1,), (0,)))
                high, low = split(middle)
                place = rows, pl.ds(WIDE * (u - 1), WIDE)
                mid_high[place] = high
                mid_low[place] = low
        rows = pl.ds(RANK * start, RANK * len(offsets))
        lhs = basis[rows, :]
        return flat_dot(lhs, mid_high[rows, :], ((0,), (0,))) + flat_dot(lhs, mid_low[rows, :], ((0,), (0,)))

    wait(zin.at[pl.ds(0, 4)], f_sem.at[F_SLOT[1]])
    out[...] = products(NEAR, 0)
    wait(zin.at[pl.ds(0, 2)], f_sem.at[F_SLOT[3]])
    out[...] += products(FAR, len(NEAR))
    wait(zin.at[0], f_sem.at[F_SLOT[4]])
    out[...] += products((4,), len(NEAR) + len(FAR))

    wait_sent(lown.at[0], 1)
    wait_sent(lx, 2)
    wait_sent(ly, 3)
    wait_sent(ly, 4)
    wait_sent(lx, 5)
    wait_sent(lown.at[0], 6)
    wait_sent(zin, 0)
    wait_sent(zout, 7)
    wait_sent(zin.at[pl.ds(0, 6)], 8)
    wait_sent(zout, 9)
    wait_sent(zin.at[pl.ds(0, 2)], 10)


def shards(
    contribution, left_basis, left_coef, right_coef, right_basis,
    left_rank, left_scale, right_rank, right_scale, left_owner, right_owner,
):
    smem = pl.BlockSpec(memory_space=pltpu.SMEM)
    hbm = pl.BlockSpec(memory_space=pl.ANY)
    unit = (RANK, WIDE)
    update = pl.pallas_call(
        kernel,
        out_shape=pltpu.VMEM((ROWS_OUT, COLS_OUT), F32),
        in_specs=[smem] * 6 + [hbm] * 4,
        out_specs=pl.BlockSpec(memory_space=pltpu.VMEM),
        scratch_shapes=[
            pltpu.VMEM((PANELS, 4) + unit, BF16),
            pltpu.VMEM((ZS, 2) + unit, BF16),
            pltpu.VMEM((ZS - 1, 2) + unit, BF16),
            pltpu.VMEM((ZS, 2) + unit, BF16),
            pltpu.VMEM((PANELS, 4) + unit, BF16),
            pltpu.VMEM((2, PANELS) + unit, BF16),
            pltpu.VMEM((PANELS,) + unit, BF16),
            pltpu.VMEM((XS, 2) + unit, BF16),
            pltpu.VMEM((3, 2) + unit, BF16),
            pltpu.VMEM((HS, 32, WIDE), BF16),
            pltpu.VMEM((3, 32, WIDE), BF16),
            pltpu.VMEM((2, XS, HS, 32, WIDE), BF16),
            pltpu.VMEM((PANELS * RANK, WIDE), BF16),
            pltpu.VMEM((PANELS * RANK, COLS_OUT), BF16),
            pltpu.VMEM((PANELS * RANK, COLS_OUT), BF16),
            pltpu.SemaphoreType.DMA((6,)),
            pltpu.SemaphoreType.DMA((11,)),
            pltpu.SemaphoreType.DMA((ZS, 2)),
            pltpu.SemaphoreType.DMA,
            pltpu.SemaphoreType.DMA((ZS, 2)),
            pltpu.SemaphoreType.DMA((4,)),
            pltpu.SemaphoreType.DMA((8,)),
        ],
        compiler_params=pltpu.CompilerParams(collective_id=0, has_side_effects=True),
    )(
        left_owner, right_owner, left_rank.T, left_scale.T, right_rank.T, right_scale.T,
        left_basis, left_coef, right_coef, right_basis,
    )
    return contribution - update


def solution(mesh):
    return jax.shard_map(
        shards,
        mesh=mesh,
        in_specs=(
            P("row", "col"),
            P(None, "col", None, "row"),
            P(None, "col", None, "row"),
            P(None, "row", None, "col"),
            P(None, "row", None, "col"),
            P(None, "row"),
            P(None, "row"),
            P(None, "col"),
            P(None, "col"),
            P(),
            P(),
        ),
        out_specs=P("row", "col"),
        check_vma=False,
    )
```

```python
import jax
import jax.numpy as jnp
from jax import lax
from jax.experimental import pallas as pl
from jax.experimental.pallas import tpu as pltpu
from jax.sharding import PartitionSpec as P

MESH = pl.DeviceIdType.MESH
BF16, F32 = jnp.bfloat16, jnp.float32
PANELS, RANK, WIDE = 8, 64, 256
ROWS_OUT, COLS_OUT = 256, 768
ZS, XS, HS = 8, 4, 4
FAR_FIRST = (4, 3, 5, 2, 6)
NEAR, FAR = (0, 1, 7, 2, 6), (3, 5)
F_SLOT = {0: 0, 1: 1, 2: 1, 6: 1, 3: 2, 5: 2, 4: 3}
G_SLOT = {(6, 0): 0, (6, 1): 1, (2, 0): 2, (2, 1): 3, (5, 0): 5, (5, 1): 6, (3, 0): 7, (3, 1): 8}
SENT = 91


def ring(value, size):
    return lax.rem(value + 4 * size, size)


def flat_dot(left, right, dims):
    return lax.dot_general(left, right, (dims, ((), ())), preferred_element_type=F32)


def split(value):
    high = value.astype(BF16)
    return high, (value - high.astype(F32)).astype(BF16)


def kernel(
    lowner, rowner, lrank, lscale, rrank, rscale,
    lbasis, lcoef, rcoef, rbasis,
    out,
    own, yin, zout, passed, zin, near, hout, hin, right,
    lown, lother, lpick, lx, lhome, ly, left,
    basis, mid_high, mid_low, all_sent,
    load_sem, send_sem, y_sem, p_sem, z_sem, n_sem, g_sem, f_sem, l_sem,
):
    row, col = lax.axis_index("row"), lax.axis_index("col")
    z, q = row // 2, lax.rem(row, 2)
    x, h, core = col // 8, lax.rem(col // 2, 4), lax.rem(col, 2)

    def at_z(offset):
        return (ring(z + offset, ZS) * 2 + q, col)

    def at_col(xx, hh, cc):
        return (row, (xx * 4 + hh) * 2 + cc)

    y_mate, core_mate = (z * 2 + 1 - q, col), at_col(x, h, 1 - core)
    x_peers = [at_col(ring(x + d, XS), h, core) for d in (1, 2, 3)]
    h_peers = [at_col(x, ring(h + d, HS), core) for d in (1, 2, 3)]
    everyone = [at_z(o) for o in FAR_FIRST + (1, 7)] + [y_mate, core_mate] + x_peers + h_peers

    for u in (1, 2, 3):
        columns = pl.ds(WIDE * (u - 1), WIDE)
        pltpu.make_async_copy(rbasis.at[:, 0, :, columns], own.at[:, u], load_sem.at[0]).start()
    pltpu.make_async_copy(rcoef.at[:, 0], own.at[:, 0], load_sem.at[0]).start()
    pltpu.make_async_copy(lbasis.at[:, 0], lown.at[0], load_sem.at[1]).start()
    pltpu.make_async_copy(lcoef.at[:, 0], lown.at[1], load_sem.at[1]).start()

    barrier = pltpu.get_barrier_semaphore()
    for peer in everyone:
        pl.semaphore_signal(barrier, inc=1, device_id=peer, device_id_type=MESH)

    def send(src, dst, sem, peer):
        pltpu.make_async_remote_copy(
            src_ref=src, dst_ref=dst, send_sem=send_sem,
            recv_sem=sem, device_id=peer, device_id_type=MESH,
        ).start()

    def wait(ref, sem):
        pltpu.make_async_remote_copy(
            src_ref=ref, dst_ref=ref, send_sem=send_sem,
            recv_sem=sem, device_id=core_mate, device_id_type=MESH,
        ).wait_recv()

    stay, leave = pl.ds(2 * q, 2), pl.ds(2 * (1 - q), 2)

    def left_core():
        send(lown.at[1 - core], lother, l_sem.at[0], core_mate)

    def left_x():
        wait(lother, l_sem.at[0])
        for p in range(PANELS):
            mine = lax.rem(lowner[p], 2) == core
            lpick[p // 2, p % 2] = jnp.where(mine, lown[core, p], lother[p])
        for d in (2, 1, 3):
            send(lpick.at[ring(x + d, XS)], lx.at[d - 1], l_sem.at[1], x_peers[d - 1])

    def left_h():
        wait(lx, l_sem.at[1])
        for i in range(2):
            away = ring(x - lowner[2 * x + i] // 8, XS)
            value = lpick[x, i]
            for d in (1, 2, 3):
                value = jnp.where(away == d, lx[d - 1, i], value)
            for j in range(2):
                lhome[2 * i + j] = value[32 * j:32 * (j + 1)]
        for d in (2, 1, 3):
            send(lhome.at[ring(h + d, HS)], ly.at[d - 1], l_sem.at[2], h_peers[d - 1])

    def left_hback():
        wait(ly, l_sem.at[2])
        away = ring(h - lax.rem(lowner[2 * x + h // 2] // 2, 4), HS)
        value = lhome[h]
        for d in (1, 2, 3):
            value = jnp.where(away == d, ly[d - 1], value)
        left[core, x, h] = value
        ref = left.at[core, x, h]
        for d in (2, 1, 3):
            send(ref, ref, l_sem.at[3], h_peers[d - 1])

    def left_xback():
        wait(ly, l_sem.at[3])
        ref = left.at[core, x]
        for d in (2, 1, 3):
            send(ref, ref, l_sem.at[4], x_peers[d - 1])
        send(ref, ref, l_sem.at[5], core_mate)

    def left_coreback():
        wait(lx, l_sem.at[4])
        for d in (1, 3, 2):
            ref = left.at[core, ring(x - d, XS)]
            send(ref, ref, l_sem.at[5], core_mate)

    def left_end():
        wait(lown.at[0], l_sem.at[5])

    def keep_at(offset, e):
        return right.at[ring(z + offset, ZS), 2 * q + e]

    def paired(offset):
        panel, slot = ring(z + offset, ZS), FAR_FIRST.index(offset)
        wait(yin.at[slot], y_sem.at[slot])
        mine = lax.rem(rowner[panel], 2) == q
        return jnp.where(mine, own[panel, stay], yin[slot])

    def begin(offset):
        slot = FAR_FIRST.index(offset)
        zout[slot] = paired(offset)
        if offset == 4:
            for e, to in ((0, 2), (1, -2)):
                send(zout.at[slot, e], passed.at[e, 2], p_sem.at[e], at_z(to))
        else:
            way, to = (0, 1) if offset == 3 else (1, -1)
            send(zout.at[slot], passed.at[way, pl.ds(0, 2)], p_sem.at[way], at_z(to))

    def merge(way):
        offset = (2, 6)[way]
        slot = FAR_FIRST.index(offset)
        panel = ring(z + offset, ZS)
        value = paired(offset)
        wait(passed.at[way], p_sem.at[way])
        away = ring(panel - rowner[panel] // 2, ZS)
        value = jnp.where(away == (3, 5)[way], passed[way, 0:2], value)
        zout[slot] = value
        zout[slot, way] = jnp.where(away == 4, passed[way, 2], value[way])
        for e in (way, 1 - way):
            send(zout.at[slot, e], zin.at[way, e], z_sem, at_z((2, -2)[way]))

    source = ring(z - rowner[z] // 2, ZS)

    def near_pick(units):
        value = jnp.where(source == 1, near[0, units], own[z, units])
        return jnp.where(source == 7, near[1, units], value)

    def relay(offset, e, to):
        ref = keep_at(offset, e)
        there = (offset - to) % ZS
        slot = 4 if there in (1, 7) else 9 if there == 4 else G_SLOT[there, e]
        send(ref, ref, g_sem.at[slot], at_z(to))

    def forward(offset, e):
        ref = keep_at(offset, e)
        send(ref, ref, f_sem.at[F_SLOT[offset]], y_mate)

    def received(offset, e):
        wait(keep_at(offset, e), g_sem.at[G_SLOT[offset, e]])

    wait(own, load_sem.at[0])
    pl.semaphore_wait(barrier, len(everyone))
    for slot, o in enumerate(FAR_FIRST):
        send(own.at[ring(z + o, ZS), leave], yin.at[slot], y_sem.at[slot], y_mate)
    for i, d in enumerate((1, -1)):
        panel = ring(z + d, ZS)
        for units in (leave, stay):
            send(own.at[panel, units], near.at[i, units], n_sem.at[0], at_z(d))
    wait(lown, load_sem.at[1])
    left_core()
    left_x()
    for o in FAR_FIRST[:3]:
        begin(o)
    wait(near, n_sem.at[0])
    hout[...] = near_pick(leave)
    send(hout, hin, n_sem.at[1], y_mate)
    left_h()
    merge(0)
    merge(1)
    wait(hin, n_sem.at[1])
    close = jnp.where(lax.rem(rowner[z], 2) == q, near_pick(stay), hin[...])
    left_hback()
    wait(zin, z_sem)
    for e in (0, 1):
        below = (source == 2) | (source == 3) | ((source == 4) & (e == 0))
        above = (source == 5) | (source == 6) | ((source == 4) & (e == 1))
        value = jnp.where(below, zin[0, e], jnp.where(above, zin[1, e], close[e]))
        right[z, 2 * q + e] = value
    for e in (0, 1):
        forward(0, e)
        relay(0, e, 2)
        relay(0, 1 - e, -2)
    for e in (0, 1):
        relay(0, e, 1)
        relay(0, 1 - e, -1)
    left_xback()
    for turn in (0, 1):
        for o, step, e in ((6, 1, turn), (2, -1, 1 - turn)):
            received(o, e)
            if turn == 0:
                relay(o, e, 2 * step)
            relay(o, e, step)
            forward(o, e)
    other = right.at[z, leave]
    wait(other, f_sem.at[F_SLOT[0]])
    for d in (1, -1):
        send(other, other, f_sem.at[F_SLOT[1]], at_z(d))
    left_coreback()
    for turn in (0, 1):
        for o, e in ((5, turn), (3, 1 - turn)):
            received(o, e)
            forward(o, e)
    wait(hin, g_sem.at[9])
    for e in (0, 1):
        forward(4, e)
    wait(own.at[0], g_sem.at[4])
    left_end()

    slot_row = lax.broadcasted_iota(jnp.int32, (RANK, RANK), 0)
    slot_col = lax.broadcasted_iota(jnp.int32, (RANK, RANK), 1)

    def products(offsets, start):
        for i, o in enumerate(offsets):
            p = ring(z + o, ZS)
            pair = p // 2, pl.ds(2 * lax.rem(p, 2), 2)
            rows = pl.ds(RANK * (start + i), RANK)
            basis[rows, :] = left[(0,) + pair].reshape(RANK, WIDE)
            coef = left[(1,) + pair].reshape(RANK, WIDE)
            small = flat_dot(coef, right[p, 0], ((1,), (1,)))
            keep = (slot_row < lrank[0, p]) & (slot_col < rrank[0, p])
            small = jnp.where(keep, small * (lscale[0, p] * rscale[0, p]), 0.0)
            small_high, small_low = split(small)
            for u in (1, 2, 3):
                wide = right[p, u]
                middle = flat_dot(small_high, wide, ((1,), (0,))) + flat_dot(small_low, wide, ((1,), (0,)))
                high, low = split(middle)
                place = rows, pl.ds(WIDE * (u - 1), WIDE)
                mid_high[place] = high
                mid_low[place] = low
        rows = pl.ds(RANK * start, RANK * len(offsets))
        lhs = basis[rows, :]
        return flat_dot(lhs, mid_high[rows, :], ((0,), (0,))) + flat_dot(lhs, mid_low[rows, :], ((0,), (0,)))

    wait(own.at[pl.ds(0, 2)], f_sem.at[F_SLOT[1]])
    out[...] = products(NEAR, 0)
    wait(own.at[0], f_sem.at[F_SLOT[3]])
    out[...] += products(FAR, len(NEAR))
    wait(hin, f_sem.at[F_SLOT[4]])
    out[...] += products((4,), len(NEAR) + len(FAR))

    pltpu.make_async_remote_copy(
        src_ref=all_sent, dst_ref=all_sent, send_sem=send_sem,
        recv_sem=z_sem, device_id=core_mate, device_id_type=MESH,
    ).wait_send()


def shards(
    contribution, left_basis, left_coef, right_coef, right_basis,
    left_rank, left_scale, right_rank, right_scale, left_owner, right_owner,
):
    smem = pl.BlockSpec(memory_space=pltpu.SMEM)
    hbm = pl.BlockSpec(memory_space=pl.ANY)
    unit = (RANK, WIDE)
    update = pl.pallas_call(
        kernel,
        out_shape=pltpu.VMEM((ROWS_OUT, COLS_OUT), F32),
        in_specs=[smem] * 6 + [hbm] * 4,
        out_specs=pl.BlockSpec(memory_space=pltpu.VMEM),
        scratch_shapes=[
            pltpu.VMEM((PANELS, 4) + unit, BF16),
            pltpu.VMEM((5, 2) + unit, BF16),
            pltpu.VMEM((5, 2) + unit, BF16),
            pltpu.VMEM((2, 3) + unit, BF16),
            pltpu.VMEM((2, 2) + unit, BF16),
            pltpu.VMEM((2, 4) + unit, BF16),
            pltpu.VMEM((2,) + unit, BF16),
            pltpu.VMEM((2,) + unit, BF16),
            pltpu.VMEM((PANELS, 4) + unit, BF16),
            pltpu.VMEM((2, PANELS) + unit, BF16),
            pltpu.VMEM((PANELS,) + unit, BF16),
            pltpu.VMEM((XS, 2) + unit, BF16),
            pltpu.VMEM((3, 2) + unit, BF16),
            pltpu.VMEM((HS, 32, WIDE), BF16),
            pltpu.VMEM((3, 32, WIDE), BF16),
            pltpu.VMEM((2, XS, HS, 32, WIDE), BF16),
            pltpu.VMEM((PANELS * RANK, WIDE), BF16),
            pltpu.VMEM((PANELS * RANK, COLS_OUT), BF16),
            pltpu.VMEM((PANELS * RANK, COLS_OUT), BF16),
            pltpu.VMEM((SENT,) + unit, BF16),
            pltpu.SemaphoreType.DMA((2,)),
            pltpu.SemaphoreType.DMA,
            pltpu.SemaphoreType.DMA((5,)),
            pltpu.SemaphoreType.DMA((2,)),
            pltpu.SemaphoreType.DMA,
            pltpu.SemaphoreType.DMA((2,)),
            pltpu.SemaphoreType.DMA((10,)),
            pltpu.SemaphoreType.DMA((4,)),
            pltpu.SemaphoreType.DMA((6,)),
        ],
        compiler_params=pltpu.CompilerParams(collective_id=0, has_side_effects=True),
    )(
        left_owner, right_owner, left_rank.T, left_scale.T, right_rank.T, right_scale.T,
        left_basis, left_coef, right_coef, right_basis,
    )
    return contribution - update


def solution(mesh):
    return jax.shard_map(
        shards,
        mesh=mesh,
        in_specs=(
            P("row", "col"),
            P(None, "col", None, "row"),
            P(None, "col", None, "row"),
            P(None, "row", None, "col"),
            P(None, "row", None, "col"),
            P(None, "row"),
            P(None, "row"),
            P(None, "col"),
            P(None, "col"),
            P(),
            P(),
        ),
        out_specs=P("row", "col"),
        check_vma=False,
    )
```

```python
import jax
import jax.numpy as jnp
from jax import lax
from jax.experimental import pallas as pl
from jax.experimental.pallas import tpu as pltpu
from jax.sharding import PartitionSpec as P

MESH = pl.DeviceIdType.MESH
BF16, F32 = jnp.bfloat16, jnp.float32
PANELS, RANK, WIDE = 8, 64, 256
ROWS_OUT, COLS_OUT = 256, 768
ZS, XS, HS = 8, 4, 4
FAR_FIRST = (4, 3, 5, 2, 6)
NEAR, FAR = (0, 1, 7, 2, 6), (3, 5)
F_SLOT = {0: 0, 1: 1, 2: 1, 6: 1, 3: 2, 5: 2, 4: 3}
G_SLOT = {(6, 0): 0, (6, 1): 1, (2, 0): 2, (2, 1): 3, (5, 0): 5, (5, 1): 6, (3, 0): 7, (3, 1): 8}
SENT = 91


def ring(value, size):
    return lax.rem(value + 4 * size, size)


def flat_dot(left, right, dims):
    return lax.dot_general(left, right, (dims, ((), ())), preferred_element_type=F32)


def split(value):
    high = value.astype(BF16)
    return high, (value - high.astype(F32)).astype(BF16)


def kernel(
    lowner, rowner, lrank, lscale, rrank, rscale,
    lbasis, lcoef, rcoef, rbasis,
    out,
    own, yin, zout, passed, zin, near, hout, hin, right,
    lown, lother, lpick, lx, lhome, ly, left,
    basis, mid_high, mid_low, all_sent,
    load_sem, send_sem, y_sem, p_sem, z_sem, n_sem, g_sem, f_sem, l_sem, h_sem,
):
    row, col = lax.axis_index("row"), lax.axis_index("col")
    z, q = row // 2, lax.rem(row, 2)
    x, h, core = col // 8, lax.rem(col // 2, 4), lax.rem(col, 2)

    def at_z(offset):
        return (ring(z + offset, ZS) * 2 + q, col)

    def at_col(xx, hh, cc):
        return (row, (xx * 4 + hh) * 2 + cc)

    y_mate, core_mate = (z * 2 + 1 - q, col), at_col(x, h, 1 - core)
    x_peers = [at_col(ring(x + d, XS), h, core) for d in (1, 2, 3)]
    h_peers = [at_col(x, ring(h + d, HS), core) for d in (1, 2, 3)]
    everyone = [at_z(o) for o in (1, -1, 2, -2)] + [y_mate, core_mate] + x_peers + [h_peers[0], h_peers[2]]

    for u in (1, 2, 3):
        columns = pl.ds(WIDE * (u - 1), WIDE)
        pltpu.make_async_copy(rbasis.at[:, 0, :, columns], own.at[:, u], load_sem.at[0]).start()
    pltpu.make_async_copy(rcoef.at[:, 0], own.at[:, 0], load_sem.at[0]).start()
    pltpu.make_async_copy(lbasis.at[:, 0], lown.at[0], load_sem.at[1]).start()
    pltpu.make_async_copy(lcoef.at[:, 0], lown.at[1], load_sem.at[1]).start()

    barrier = pltpu.get_barrier_semaphore()
    for peer in everyone:
        pl.semaphore_signal(barrier, inc=1, device_id=peer, device_id_type=MESH)

    def send(src, dst, sem, peer):
        pltpu.make_async_remote_copy(
            src_ref=src, dst_ref=dst, send_sem=send_sem,
            recv_sem=sem, device_id=peer, device_id_type=MESH,
        ).start()

    def wait(ref, sem):
        pltpu.make_async_remote_copy(
            src_ref=ref, dst_ref=ref, send_sem=send_sem,
            recv_sem=sem, device_id=core_mate, device_id_type=MESH,
        ).wait_recv()

    stay, leave = pl.ds(2 * q, 2), pl.ds(2 * (1 - q), 2)

    def left_core():
        send(lown.at[1 - core], lother, l_sem.at[0], core_mate)

    def left_x():
        wait(lother, l_sem.at[0])
        for p in range(PANELS):
            mine = lax.rem(lowner[p], 2) == core
            lpick[p // 2, p % 2] = jnp.where(mine, lown[core, p], lother[p])
        for d in (2, 1, 3):
            send(lpick.at[ring(x + d, XS)], lx.at[d - 1], l_sem.at[1], x_peers[d - 1])

    def left_h():
        wait(lx, l_sem.at[1])
        pl.semaphore_wait(h_sem, 1)
        for i in range(2):
            away = ring(x - lowner[2 * x + i] // 8, XS)
            value = lpick[x, i]
            for d in (1, 2, 3):
                value = jnp.where(away == d, lx[d - 1, i], value)
            for j in range(2):
                lhome[2 * i + j] = value[32 * j:32 * (j + 1)]
        for d in (2, 1, 3):
            send(lhome.at[ring(h + d, HS)], ly.at[d - 1], l_sem.at[2], h_peers[d - 1])

    def left_hback():
        wait(ly, l_sem.at[2])
        away = ring(h - lax.rem(lowner[2 * x + h // 2] // 2, 4), HS)
        value = lhome[h]
        for d in (1, 2, 3):
            value = jnp.where(away == d, ly[d - 1], value)
        left[core, x, h] = value
        ref = left.at[core, x, h]
        for d in (2, 1, 3):
            send(ref, ref, l_sem.at[3], h_peers[d - 1])

    def left_xback():
        wait(ly, l_sem.at[3])
        ref = left.at[core, x]
        for d in (2, 1, 3):
            send(ref, ref, l_sem.at[4], x_peers[d - 1])
        send(ref, ref, l_sem.at[5], core_mate)

    def left_coreback():
        wait(lx, l_sem.at[4])
        for d in (1, 3, 2):
            ref = left.at[core, ring(x - d, XS)]
            send(ref, ref, l_sem.at[5], core_mate)

    def left_end():
        wait(lown.at[0], l_sem.at[5])

    def keep_at(offset, e):
        return right.at[ring(z + offset, ZS), 2 * q + e]

    def swap(offset):
        slot = FAR_FIRST.index(offset)
        for e in (0, 1):
            unit = own.at[ring(z + offset, ZS), 2 * (1 - q) + e]
            send(unit, yin.at[slot, e], y_sem.at[slot, e], y_mate)

    def paired(offset, e):
        panel, slot = ring(z + offset, ZS), FAR_FIRST.index(offset)
        wait(yin.at[slot, e], y_sem.at[slot, e])
        mine = lax.rem(rowner[panel], 2) == q
        return jnp.where(mine, own[panel, 2 * q + e], yin[slot, e])

    def begin(offset):
        slot = FAR_FIRST.index(offset)
        for e in (0, 1) if offset != 5 else (1, 0):
            zout[slot, e] = paired(offset, e)
            way = e if offset == 4 else 0 if offset == 3 else 1
            place = 2 if offset == 4 else int(e == way)
            far = 2 if offset == 4 else 1
            send(zout.at[slot, e], passed.at[way, place], p_sem.at[way, int(e == way)], at_z((far, -far)[way]))

    def merge(e):
        for way, unit in ((0, e), (1, 1 - e)):
            offset = (2, 6)[way]
            slot = FAR_FIRST.index(offset)
            panel = ring(z + offset, ZS)
            value = paired(offset, unit)
            away = ring(panel - rowner[panel] // 2, ZS)
            if unit == way:
                wait(passed.at[way, pl.ds(1, 2)], p_sem.at[way, 1])
                value = jnp.where(away == (3, 5)[way], passed[way, 1], value)
                value = jnp.where(away == 4, passed[way, 2], value)
            else:
                wait(passed.at[way, 0], p_sem.at[way, 0])
                value = jnp.where(away == (3, 5)[way], passed[way, 0], value)
            zout[slot, unit] = value
            send(zout.at[slot, unit], zin.at[way, unit], z_sem, at_z((2, -2)[way]))

    source = ring(z - rowner[z] // 2, ZS)

    def near_pick(units):
        value = jnp.where(source == 1, near[0, units], own[z, units])
        return jnp.where(source == 7, near[1, units], value)

    def relay(offset, e, to):
        ref = keep_at(offset, e)
        there = (offset - to) % ZS
        slot = 4 if there in (1, 7) else 9 if there == 4 else G_SLOT[there, e]
        send(ref, ref, g_sem.at[slot], at_z(to))

    def forward(offset, e):
        ref = keep_at(offset, e)
        send(ref, ref, f_sem.at[F_SLOT[offset]], y_mate)

    def received(offset, e):
        wait(keep_at(offset, e), g_sem.at[G_SLOT[offset, e]])

    wait(own, load_sem.at[0])
    pl.semaphore_wait(barrier, len(everyone))
    pl.semaphore_signal(h_sem, inc=1, device_id=h_peers[0], device_id_type=MESH)
    for o in FAR_FIRST[:3]:
        swap(o)
    for i, d in enumerate((1, -1)):
        panel = ring(z + d, ZS)
        for units in (leave, stay):
            send(own.at[panel, units], near.at[i, units], n_sem.at[0], at_z(d))
    wait(lown, load_sem.at[1])
    left_core()
    left_x()
    begin(FAR_FIRST[0])
    for o in FAR_FIRST[3:]:
        swap(o)
    for o in FAR_FIRST[1:3]:
        begin(o)
    wait(near, n_sem.at[0])
    hout[...] = near_pick(leave)
    send(hout, hin, n_sem.at[1], y_mate)
    left_h()
    merge(0)
    merge(1)
    wait(hin, n_sem.at[1])
    close = jnp.where(lax.rem(rowner[z], 2) == q, near_pick(stay), hin[...])
    left_hback()
    wait(zin, z_sem)
    for e in (0, 1):
        below = (source == 2) | (source == 3) | ((source == 4) & (e == 0))
        above = (source == 5) | (source == 6) | ((source == 4) & (e == 1))
        value = jnp.where(below, zin[0, e], jnp.where(above, zin[1, e], close[e]))
        right[z, 2 * q + e] = value
    for e in (0, 1):
        forward(0, e)
        relay(0, e, 2)
        relay(0, 1 - e, -2)
    left_xback()
    for turn in (0, 1):
        for o, step, e in ((6, 1, turn), (2, -1, 1 - turn)):
            received(o, e)
            if turn == 0:
                relay(o, e, 2 * step)
            relay(o, e, step)
            forward(o, e)
    for e in (0, 1):
        relay(0, e, 1)
        relay(0, 1 - e, -1)
    other = right.at[z, leave]
    wait(other, f_sem.at[F_SLOT[0]])
    for d in (1, -1):
        send(other, other, f_sem.at[F_SLOT[1]], at_z(d))
    left_coreback()
    for turn in (0, 1):
        for o, e in ((5, turn), (3, 1 - turn)):
            received(o, e)
            forward(o, e)
    wait(hin, g_sem.at[9])
    for e in (0, 1):
        forward(4, e)
    wait(own.at[0], g_sem.at[4])
    left_end()

    slot_row = lax.broadcasted_iota(jnp.int32, (RANK, RANK), 0)
    slot_col = lax.broadcasted_iota(jnp.int32, (RANK, RANK), 1)

    def products(offsets, start):
        for i, o in enumerate(offsets):
            p = ring(z + o, ZS)
            pair = p // 2, pl.ds(2 * lax.rem(p, 2), 2)
            rows = pl.ds(RANK * (start + i), RANK)
            basis[rows, :] = left[(0,) + pair].reshape(RANK, WIDE)
            coef = left[(1,) + pair].reshape(RANK, WIDE)
            small = flat_dot(coef, right[p, 0], ((1,), (1,)))
            keep = (slot_row < lrank[0, p]) & (slot_col < rrank[0, p])
            small = jnp.where(keep, small * (lscale[0, p] * rscale[0, p]), 0.0)
            small_high, small_low = split(small)
            for u in (1, 2, 3):
                wide = right[p, u]
                middle = flat_dot(small_high, wide, ((1,), (0,))) + flat_dot(small_low, wide, ((1,), (0,)))
                high, low = split(middle)
                place = rows, pl.ds(WIDE * (u - 1), WIDE)
                mid_high[place] = high
                mid_low[place] = low
        rows = pl.ds(RANK * start, RANK * len(offsets))
        lhs = basis[rows, :]
        return flat_dot(lhs, mid_high[rows, :], ((0,), (0,))) + flat_dot(lhs, mid_low[rows, :], ((0,), (0,)))

    wait(own.at[pl.ds(0, 2)], f_sem.at[F_SLOT[1]])
    out[...] = products(NEAR, 0)
    wait(own.at[0], f_sem.at[F_SLOT[3]])
    out[...] += products(FAR, len(NEAR))
    wait(hin, f_sem.at[F_SLOT[4]])
    out[...] += products((4,), len(NEAR) + len(FAR))

    pltpu.make_async_remote_copy(
        src_ref=all_sent, dst_ref=all_sent, send_sem=send_sem,
        recv_sem=z_sem, device_id=core_mate, device_id_type=MESH,
    ).wait_send()


def shards(
    contribution, left_basis, left_coef, right_coef, right_basis,
    left_rank, left_scale, right_rank, right_scale, left_owner, right_owner,
):
    smem = pl.BlockSpec(memory_space=pltpu.SMEM)
    hbm = pl.BlockSpec(memory_space=pl.ANY)
    unit = (RANK, WIDE)
    update = pl.pallas_call(
        kernel,
        out_shape=pltpu.VMEM((ROWS_OUT, COLS_OUT), F32),
        in_specs=[smem] * 6 + [hbm] * 4,
        out_specs=pl.BlockSpec(memory_space=pltpu.VMEM),
        scratch_shapes=[
            pltpu.VMEM((PANELS, 4) + unit, BF16),
            pltpu.VMEM((5, 2) + unit, BF16),
            pltpu.VMEM((5, 2) + unit, BF16),
            pltpu.VMEM((2, 3) + unit, BF16),
            pltpu.VMEM((2, 2) + unit, BF16),
            pltpu.VMEM((2, 4) + unit, BF16),
            pltpu.VMEM((2,) + unit, BF16),
            pltpu.VMEM((2,) + unit, BF16),
            pltpu.VMEM((PANELS, 4) + unit, BF16),
            pltpu.VMEM((2, PANELS) + unit, BF16),
            pltpu.VMEM((PANELS,) + unit, BF16),
            pltpu.VMEM((XS, 2) + unit, BF16),
            pltpu.VMEM((3, 2) + unit, BF16),
            pltpu.VMEM((HS, 32, WIDE), BF16),
            pltpu.VMEM((3, 32, WIDE), BF16),
            pltpu.VMEM((2, XS, HS, 32, WIDE), BF16),
            pltpu.VMEM((PANELS * RANK, WIDE), BF16),
            pltpu.VMEM((PANELS * RANK, COLS_OUT), BF16),
            pltpu.VMEM((PANELS * RANK, COLS_OUT), BF16),
            pltpu.VMEM((SENT,) + unit, BF16),
            pltpu.SemaphoreType.DMA((2,)),
            pltpu.SemaphoreType.DMA,
            pltpu.SemaphoreType.DMA((5, 2)),
            pltpu.SemaphoreType.DMA((2, 2)),
            pltpu.SemaphoreType.DMA,
            pltpu.SemaphoreType.DMA((2,)),
            pltpu.SemaphoreType.DMA((10,)),
            pltpu.SemaphoreType.DMA((4,)),
            pltpu.SemaphoreType.DMA((6,)),
            pltpu.SemaphoreType.REGULAR,
        ],
        compiler_params=pltpu.CompilerParams(collective_id=0, has_side_effects=True),
    )(
        left_owner, right_owner, left_rank.T, left_scale.T, right_rank.T, right_scale.T,
        left_basis, left_coef, right_coef, right_basis,
    )
    return contribution - update


def solution(mesh):
    return jax.shard_map(
        shards,
        mesh=mesh,
        in_specs=(
            P("row", "col"),
            P(None, "col", None, "row"),
            P(None, "col", None, "row"),
            P(None, "row", None, "col"),
            P(None, "row", None, "col"),
            P(None, "row"),
            P(None, "row"),
            P(None, "col"),
            P(None, "col"),
            P(),
            P(),
        ),
        out_specs=P("row", "col"),
        check_vma=False,
    )
```

```python
import jax
import jax.numpy as jnp
from jax import lax
from jax.experimental import pallas as pl
from jax.experimental.pallas import tpu as pltpu
from jax.sharding import PartitionSpec as P

MESH = pl.DeviceIdType.MESH
BF16, F32 = jnp.bfloat16, jnp.float32
PANELS, RANK, WIDE = 8, 64, 256
ROWS_OUT, COLS_OUT = 256, 768
ZS, XS, HS = 8, 4, 4
FAR_FIRST = (4, 3, 5, 2, 6)
NEAR, FAR = (0, 1, 7, 2, 6), (3, 5)
F_SLOT = {0: 0, 1: 1, 2: 1, 6: 1, 3: 2, 5: 2, 4: 3}
G_SLOT = {(6, 0): 0, (6, 1): 1, (2, 0): 2, (2, 1): 3, (5, 0): 5, (5, 1): 6, (3, 0): 7, (3, 1): 8}
SENT = 91


def ring(value, size):
    return lax.rem(value + 4 * size, size)


def flat_dot(left, right, dims):
    return lax.dot_general(left, right, (dims, ((), ())), preferred_element_type=F32)


def split(value):
    high = value.astype(BF16)
    return high, (value - high.astype(F32)).astype(BF16)


def kernel(
    lowner, rowner, lrank, lscale, rrank, rscale,
    lbasis, lcoef, rcoef, rbasis,
    out,
    own, yin, zout, passed, zin, near, hout, hin, right,
    lown, lother, lpick, lx, lhome, ly, left,
    basis, mid_high, mid_low, all_sent,
    load_sem, send_sem, y_sem, p_sem, z_sem, n_sem, g_sem, f_sem, l_sem, h_sem,
):
    row, col = lax.axis_index("row"), lax.axis_index("col")
    z, q = row // 2, lax.rem(row, 2)
    x, h, core = col // 8, lax.rem(col // 2, 4), lax.rem(col, 2)

    def at_z(offset):
        return (ring(z + offset, ZS) * 2 + q, col)

    def at_col(xx, hh, cc):
        return (row, (xx * 4 + hh) * 2 + cc)

    y_mate, core_mate = (z * 2 + 1 - q, col), at_col(x, h, 1 - core)
    x_peers = [at_col(ring(x + d, XS), h, core) for d in (1, 2, 3)]
    h_peers = [at_col(x, ring(h + d, HS), core) for d in (1, 2, 3)]
    everyone = [at_z(o) for o in (1, -1, 2, -2)] + [y_mate, core_mate] + x_peers

    for u in (1, 2, 3):
        columns = pl.ds(WIDE * (u - 1), WIDE)
        pltpu.make_async_copy(rbasis.at[:, 0, :, columns], own.at[:, u], load_sem.at[0]).start()
    pltpu.make_async_copy(rcoef.at[:, 0], own.at[:, 0], load_sem.at[0]).start()
    pltpu.make_async_copy(lbasis.at[:, 0], lown.at[0], load_sem.at[1]).start()
    pltpu.make_async_copy(lcoef.at[:, 0], lown.at[1], load_sem.at[1]).start()

    def tell(sem, peer):
        pl.semaphore_signal(sem, inc=1, device_id=peer, device_id_type=MESH)

    h_next, h_last = h_peers[0], h_peers[2]
    barrier = pltpu.get_barrier_semaphore()
    for peer in everyone:
        tell(barrier, peer)

    @pl.when(h < HS - 1)
    def _():
        tell(barrier, h_next)

    @pl.when(h > 0)
    def _():
        tell(barrier, h_last)

    def send(src, dst, sem, peer):
        pltpu.make_async_remote_copy(
            src_ref=src, dst_ref=dst, send_sem=send_sem,
            recv_sem=sem, device_id=peer, device_id_type=MESH,
        ).start()

    def wait(ref, sem):
        pltpu.make_async_remote_copy(
            src_ref=ref, dst_ref=ref, send_sem=send_sem,
            recv_sem=sem, device_id=core_mate, device_id_type=MESH,
        ).wait_recv()

    stay, leave = pl.ds(2 * q, 2), pl.ds(2 * (1 - q), 2)

    def left_core():
        send(lown.at[1 - core], lother, l_sem.at[0], core_mate)

    def left_x():
        wait(lother, l_sem.at[0])
        for p in range(PANELS):
            mine = lax.rem(lowner[p], 2) == core
            lpick[p // 2, p % 2] = jnp.where(mine, lown[core, p], lother[p])
        for d in (2, 1, 3):
            send(lpick.at[ring(x + d, XS)], lx.at[d - 1], l_sem.at[1], x_peers[d - 1])

    def left_h():
        wait(lx, l_sem.at[1])

        @pl.when(jnp.logical_not(inner))
        def _():
            pl.semaphore_wait(h_sem, 2)

        for i in range(2):
            away = ring(x - lowner[2 * x + i] // 8, XS)
            value = lpick[x, i]
            for d in (1, 2, 3):
                value = jnp.where(away == d, lx[d - 1, i], value)
            for j in range(2):
                lhome[2 * i + j] = value[32 * j:32 * (j + 1)]
        for d in (2, 1, 3):
            send(lhome.at[ring(h + d, HS)], ly.at[d - 1], l_sem.at[2], h_peers[d - 1])

    def left_hback():
        wait(ly, l_sem.at[2])
        away = ring(h - lax.rem(lowner[2 * x + h // 2] // 2, 4), HS)
        value = lhome[h]
        for d in (1, 2, 3):
            value = jnp.where(away == d, ly[d - 1], value)
        left[core, x, h] = value
        ref = left.at[core, x, h]
        for d in (2, 1, 3):
            send(ref, ref, l_sem.at[3], h_peers[d - 1])

    def left_xback():
        wait(ly, l_sem.at[3])
        ref = left.at[core, x]
        for d in (2, 1, 3):
            send(ref, ref, l_sem.at[4], x_peers[d - 1])
        send(ref, ref, l_sem.at[5], core_mate)

    def left_coreback():
        wait(lx, l_sem.at[4])
        for d in (1, 3, 2):
            ref = left.at[core, ring(x - d, XS)]
            send(ref, ref, l_sem.at[5], core_mate)

    def left_end():
        wait(lown.at[0], l_sem.at[5])

    def keep_at(offset, e):
        return right.at[ring(z + offset, ZS), 2 * q + e]

    def swap(offset):
        slot = FAR_FIRST.index(offset)
        for e in (0, 1):
            unit = own.at[ring(z + offset, ZS), 2 * (1 - q) + e]
            send(unit, yin.at[slot, e], y_sem.at[slot, e], y_mate)

    def paired(offset, e):
        panel, slot = ring(z + offset, ZS), FAR_FIRST.index(offset)
        wait(yin.at[slot, e], y_sem.at[slot, e])
        mine = lax.rem(rowner[panel], 2) == q
        return jnp.where(mine, own[panel, 2 * q + e], yin[slot, e])

    def begin(offset):
        slot = FAR_FIRST.index(offset)
        for e in (0, 1) if offset != 5 else (1, 0):
            zout[slot, e] = paired(offset, e)
            way = e if offset == 4 else 0 if offset == 3 else 1
            place = 2 if offset == 4 else int(e == way)
            far = 2 if offset == 4 else 1
            send(zout.at[slot, e], passed.at[way, place], p_sem.at[way, int(e == way)], at_z((far, -far)[way]))

    def merge(e):
        for way, unit in ((0, e), (1, 1 - e)):
            offset = (2, 6)[way]
            slot = FAR_FIRST.index(offset)
            panel = ring(z + offset, ZS)
            value = paired(offset, unit)
            away = ring(panel - rowner[panel] // 2, ZS)
            if unit == way:
                wait(passed.at[way, pl.ds(1, 2)], p_sem.at[way, 1])
                value = jnp.where(away == (3, 5)[way], passed[way, 1], value)
                value = jnp.where(away == 4, passed[way, 2], value)
            else:
                wait(passed.at[way, 0], p_sem.at[way, 0])
                value = jnp.where(away == (3, 5)[way], passed[way, 0], value)
            zout[slot, unit] = value
            send(zout.at[slot, unit], zin.at[way, unit], z_sem, at_z((2, -2)[way]))

    source = ring(z - rowner[z] // 2, ZS)

    def near_pick(units):
        value = jnp.where(source == 1, near[0, units], own[z, units])
        return jnp.where(source == 7, near[1, units], value)

    def relay(offset, e, to):
        ref = keep_at(offset, e)
        there = (offset - to) % ZS
        slot = 4 if there in (1, 7) else 9 if there == 4 else G_SLOT[there, e]
        send(ref, ref, g_sem.at[slot], at_z(to))

    def forward(offset, e):
        ref = keep_at(offset, e)
        send(ref, ref, f_sem.at[F_SLOT[offset]], y_mate)

    def received(offset, e):
        wait(keep_at(offset, e), g_sem.at[G_SLOT[offset, e]])

    wait(own, load_sem.at[0])
    inner = (h > 0) & (h < HS - 1)
    pl.semaphore_wait(barrier, len(everyone) + jnp.where(inner, 2, 1))

    @pl.when(inner)
    def _():
        tell(h_sem, h_next)
        tell(h_sem, h_last)

    for o in FAR_FIRST[:3]:
        swap(o)
    for i, d in enumerate((1, -1)):
        panel = ring(z + d, ZS)
        for units in (leave, stay):
            send(own.at[panel, units], near.at[i, units], n_sem.at[0], at_z(d))
    wait(lown, load_sem.at[1])
    left_core()
    left_x()
    begin(FAR_FIRST[0])

    @pl.when(inner)
    def _():
        pl.semaphore_wait(h_sem, 1)
        tell(h_sem, (row, (x * 4 + jnp.where(h == 1, 0, HS - 1)) * 2 + core))

    for o in FAR_FIRST[3:]:
        swap(o)
    for o in FAR_FIRST[1:3]:
        begin(o)
    wait(near, n_sem.at[0])
    hout[...] = near_pick(leave)
    send(hout, hin, n_sem.at[1], y_mate)
    left_h()
    merge(0)
    merge(1)
    wait(hin, n_sem.at[1])
    close = jnp.where(lax.rem(rowner[z], 2) == q, near_pick(stay), hin[...])
    left_hback()
    wait(zin, z_sem)
    for e in (0, 1):
        below = (source == 2) | (source == 3) | ((source == 4) & (e == 0))
        above = (source == 5) | (source == 6) | ((source == 4) & (e == 1))
        value = jnp.where(below, zin[0, e], jnp.where(above, zin[1, e], close[e]))
        right[z, 2 * q + e] = value
    for e in (0, 1):
        forward(0, e)
        relay(0, e, 2)
        relay(0, 1 - e, -2)
    left_xback()
    for turn in (0, 1):
        for o, step, e in ((6, 1, turn), (2, -1, 1 - turn)):
            received(o, e)
            if turn == 0:
                relay(o, e, 2 * step)
            relay(o, e, step)
            forward(o, e)
    for e in (0, 1):
        relay(0, e, 1)
        relay(0, 1 - e, -1)
    other = right.at[z, leave]
    wait(other, f_sem.at[F_SLOT[0]])
    for d in (1, -1):
        send(other, other, f_sem.at[F_SLOT[1]], at_z(d))
    left_coreback()
    for turn in (0, 1):
        for o, e in ((5, turn), (3, 1 - turn)):
            received(o, e)
            forward(o, e)
    wait(hin, g_sem.at[9])
    for e in (0, 1):
        forward(4, e)
    wait(own.at[0], g_sem.at[4])
    left_end()

    slot_row = lax.broadcasted_iota(jnp.int32, (RANK, RANK), 0)
    slot_col = lax.broadcasted_iota(jnp.int32, (RANK, RANK), 1)

    def products(offsets, start):
        for i, o in enumerate(offsets):
            p = ring(z + o, ZS)
            pair = p // 2, pl.ds(2 * lax.rem(p, 2), 2)
            rows = pl.ds(RANK * (start + i), RANK)
            basis[rows, :] = left[(0,) + pair].reshape(RANK, WIDE)
            coef = left[(1,) + pair].reshape(RANK, WIDE)
            small = flat_dot(coef, right[p, 0], ((1,), (1,)))
            keep = (slot_row < lrank[0, p]) & (slot_col < rrank[0, p])
            small = jnp.where(keep, small * (lscale[0, p] * rscale[0, p]), 0.0)
            small_high, small_low = split(small)
            for u in (1, 2, 3):
                wide = right[p, u]
                middle = flat_dot(small_high, wide, ((1,), (0,))) + flat_dot(small_low, wide, ((1,), (0,)))
                high, low = split(middle)
                place = rows, pl.ds(WIDE * (u - 1), WIDE)
                mid_high[place] = high
                mid_low[place] = low
        rows = pl.ds(RANK * start, RANK * len(offsets))
        lhs = basis[rows, :]
        return flat_dot(lhs, mid_high[rows, :], ((0,), (0,))) + flat_dot(lhs, mid_low[rows, :], ((0,), (0,)))

    wait(own.at[pl.ds(0, 2)], f_sem.at[F_SLOT[1]])
    out[...] = products(NEAR, 0)
    wait(own.at[0], f_sem.at[F_SLOT[3]])
    out[...] += products(FAR, len(NEAR))
    wait(hin, f_sem.at[F_SLOT[4]])
    out[...] += products((4,), len(NEAR) + len(FAR))

    pltpu.make_async_remote_copy(
        src_ref=all_sent, dst_ref=all_sent, send_sem=send_sem,
        recv_sem=z_sem, device_id=core_mate, device_id_type=MESH,
    ).wait_send()


def shards(
    contribution, left_basis, left_coef, right_coef, right_basis,
    left_rank, left_scale, right_rank, right_scale, left_owner, right_owner,
):
    smem = pl.BlockSpec(memory_space=pltpu.SMEM)
    hbm = pl.BlockSpec(memory_space=pl.ANY)
    unit = (RANK, WIDE)
    update = pl.pallas_call(
        kernel,
        out_shape=pltpu.VMEM((ROWS_OUT, COLS_OUT), F32),
        in_specs=[smem] * 6 + [hbm] * 4,
        out_specs=pl.BlockSpec(memory_space=pltpu.VMEM),
        scratch_shapes=[
            pltpu.VMEM((PANELS, 4) + unit, BF16),
            pltpu.VMEM((5, 2) + unit, BF16),
            pltpu.VMEM((5, 2) + unit, BF16),
            pltpu.VMEM((2, 3) + unit, BF16),
            pltpu.VMEM((2, 2) + unit, BF16),
            pltpu.VMEM((2, 4) + unit, BF16),
            pltpu.VMEM((2,) + unit, BF16),
            pltpu.VMEM((2,) + unit, BF16),
            pltpu.VMEM((PANELS, 4) + unit, BF16),
            pltpu.VMEM((2, PANELS) + unit, BF16),
            pltpu.VMEM((PANELS,) + unit, BF16),
            pltpu.VMEM((XS, 2) + unit, BF16),
            pltpu.VMEM((3, 2) + unit, BF16),
            pltpu.VMEM((HS, 32, WIDE), BF16),
            pltpu.VMEM((3, 32, WIDE), BF16),
            pltpu.VMEM((2, XS, HS, 32, WIDE), BF16),
            pltpu.VMEM((PANELS * RANK, WIDE), BF16),
            pltpu.VMEM((PANELS * RANK, COLS_OUT), BF16),
            pltpu.VMEM((PANELS * RANK, COLS_OUT), BF16),
            pltpu.VMEM((SENT,) + unit, BF16),
            pltpu.SemaphoreType.DMA((2,)),
            pltpu.SemaphoreType.DMA,
            pltpu.SemaphoreType.DMA((5, 2)),
            pltpu.SemaphoreType.DMA((2, 2)),
            pltpu.SemaphoreType.DMA,
            pltpu.SemaphoreType.DMA((2,)),
            pltpu.SemaphoreType.DMA((10,)),
            pltpu.SemaphoreType.DMA((4,)),
            pltpu.SemaphoreType.DMA((6,)),
            pltpu.SemaphoreType.REGULAR,
        ],
        compiler_params=pltpu.CompilerParams(collective_id=0, has_side_effects=True),
    )(
        left_owner, right_owner, left_rank.T, left_scale.T, right_rank.T, right_scale.T,
        left_basis, left_coef, right_coef, right_basis,
    )
    return contribution - update


def solution(mesh):
    return jax.shard_map(
        shards,
        mesh=mesh,
        in_specs=(
            P("row", "col"),
            P(None, "col", None, "row"),
            P(None, "col", None, "row"),
            P(None, "row", None, "col"),
            P(None, "row", None, "col"),
            P(None, "row"),
            P(None, "row"),
            P(None, "col"),
            P(None, "col"),
            P(),
            P(),
        ),
        out_specs=P("row", "col"),
        check_vma=False,
    )
```
